512 devices in a mesh: ctx: 16 (over x, z_hi), fsdp: 32 (over z_lo, y, core).
Axes of the slice: x: 4, y: 4, z: 16 (z_hi: 4, z_lo: 4; z = z_hi * 4 + z_lo), core: 2. Of those that a mesh axis runs over, the one named last changes fastest.
Arguments:
- block_pos: int32 [8, 16], P(None, 'ctx'), may hold values from 0 to 15, each once within a row
- queries: bfloat16 [32, 2048, 640], P('fsdp', 'ctx'), may hold values from -6 to 6
- keys: bfloat16 [32, 2048, 128], P('fsdp', 'ctx'), may hold values from -6 to 6
- values: bfloat16 [32, 2048, 128], P('fsdp', 'ctx'), may hold values from -12 to 12
- attention_output: bfloat16 [32, 2048, 640], P('fsdp', 'ctx'), may hold values from -6 to 6
- output_gradient: bfloat16 [32, 2048, 640], P('fsdp', 'ctx'), may hold values from -24 to 24
- log_softmax_norm: float32 [32, 5, 2048], P('fsdp', None, 'ctx'), may hold values from 6 to 9
- features: bfloat16 [8, 2048, 2560], P(None, 'ctx', 'fsdp'), may hold values from -0.119628906 to 0.119628906
Outputs:
- grad_q: bfloat16 [32, 2048, 640], P('fsdp', 'ctx')
- key_gradient: bfloat16 [32, 2048, 128], P('fsdp', 'ctx')
- value_gradient: bfloat16 [32, 2048, 128], P('fsdp', 'ctx')
- grad_wk: float32 [2560, 512], P('fsdp')
The draws below stay inside these ranges and needn't reach their ends.
Inputs may be any that keep to these rules, and one draw needn't show every extreme that they name: Each row of block_pos holds every block place 0 to 15 once.
All inputs are finite; a program needn't handle non-finite values.
Results may differ from the reference program's by a relative error of at most 0.0058.
Values may be sent and summed in bfloat16 or wider, within the bound.
No kernel may reach another device: no remote copies, remote signals or barrier semaphores. Data moves between devices by JAX's collectives and lax.ppermute only.
A program may use at most 64 MiB of HBM per device.

```python
import jax
import jax.numpy as jnp
from jax import lax

QUERY_HEADS = 20
KEY_VALUE_HEADS = 4
HEAD_SIZE = 128
HEAD_GROUPS = 4
DW = 2560
BLOCK_TOKENS = 128
SEQUENCE_COUNT = 8
SEQUENCE_TOKENS = 2048
N_CTX = 16


def level_of(key, shape, pieces, low, top_value):
    factor_of = 1.0
    for axis_at, shards_of in pieces:
        draws = jax.random.uniform(jax.random.fold_in(jax.random.fold_in(key, 6), axis_at), (shards_of,), jnp.float32, low / len(pieces), top_value / len(pieces))
        factor_of = factor_of * jnp.repeat(jnp.exp(draws), shape[axis_at] // shards_of).reshape((-1,) + (1,) * (len(shape) - 1 - axis_at))
    return factor_of


def centred(stream_key, dims, width, bound, cuts=(), kind=jnp.bfloat16):
    values = width * jax.random.normal(stream_key, dims, jnp.float32)
    if cuts:
        values = values * level_of(stream_key, dims, cuts, -0.22, 0.18)
    return jnp.clip(values, -bound, bound).astype(kind)


def setup_inputs(seed: int = 0) -> dict:
    streams_of = jax.random.split(jax.random.key(seed), 9)
    return {
        "block_pos": jax.vmap(lambda own: jax.random.permutation(own, N_CTX))(jax.random.split(streams_of[0], SEQUENCE_COUNT)).reshape((SEQUENCE_COUNT, N_CTX)).astype(jnp.int32),
        "queries": centred(streams_of[1], (SEQUENCE_COUNT * HEAD_GROUPS, SEQUENCE_TOKENS, (QUERY_HEADS // HEAD_GROUPS) * HEAD_SIZE), 1.0, 6.0, ((0, 32), (1, 16))),
        "keys": centred(streams_of[2], (SEQUENCE_COUNT * HEAD_GROUPS, SEQUENCE_TOKENS, (KEY_VALUE_HEADS // HEAD_GROUPS) * HEAD_SIZE), 1.0, 6.0, ((0, 32), (1, 16))),
        "values": centred(streams_of[3], (SEQUENCE_COUNT * HEAD_GROUPS, SEQUENCE_TOKENS, (KEY_VALUE_HEADS // HEAD_GROUPS) * HEAD_SIZE), 2.0, 12.0, ((0, 32), (1, 16))),
        "attention_output": centred(streams_of[4], (SEQUENCE_COUNT * HEAD_GROUPS, SEQUENCE_TOKENS, (QUERY_HEADS // HEAD_GROUPS) * HEAD_SIZE), 1.0, 6.0, ((0, 32), (1, 16))),
        "output_gradient": centred(streams_of[5], (SEQUENCE_COUNT * HEAD_GROUPS, SEQUENCE_TOKENS, (QUERY_HEADS // HEAD_GROUPS) * HEAD_SIZE), 4.0, 24.0, ((0, 32), (1, 16))),
        "log_softmax_norm": jnp.clip(6.0 + 3.0 * jax.random.uniform(streams_of[6], (SEQUENCE_COUNT * HEAD_GROUPS, QUERY_HEADS // HEAD_GROUPS, SEQUENCE_TOKENS), jnp.float32) ** level_of(streams_of[6], (SEQUENCE_COUNT * HEAD_GROUPS, QUERY_HEADS // HEAD_GROUPS, SEQUENCE_TOKENS), ((0, 32), (2, 16)), -0.2, 0.2), 6.0, 9.0),
        "features": centred(streams_of[7], (SEQUENCE_COUNT, SEQUENCE_TOKENS, DW), 0.02, 0.119628906, ((1, 16), (2, 32))),
    }


def low_round(value):
    return lax.optimization_barrier(value.astype(jnp.bfloat16)).astype(jnp.float32)


def one_row(inputs):
    block_row, queries, keys, values, attention_output, output_gradient, log_softmax_norm = inputs
    sequence_length = queries.shape[0]
    kv_local = KEY_VALUE_HEADS // HEAD_GROUPS
    group_size = QUERY_HEADS // KEY_VALUE_HEADS
    score_scale = HEAD_SIZE ** -0.5
    offsets = jnp.arange(BLOCK_TOKENS, dtype=jnp.int32)
    positions = (block_row[:, None] * BLOCK_TOKENS + offsets[None, :]).reshape(sequence_length)
    visible = positions[None, :] <= positions[:, None]
    heads_of_queries = queries.astype(jnp.float32).reshape(sequence_length, kv_local, group_size, HEAD_SIZE).transpose(1, 0, 2, 3)
    head_gradient = output_gradient.astype(jnp.float32).reshape(sequence_length, kv_local, group_size, HEAD_SIZE).transpose(1, 0, 2, 3)
    heads_of_output = attention_output.astype(jnp.float32).reshape(sequence_length, kv_local, group_size, HEAD_SIZE).transpose(1, 0, 2, 3)
    heads_of_keys = keys.astype(jnp.float32).reshape(sequence_length, kv_local, HEAD_SIZE).transpose(1, 0, 2)
    heads_of_values = values.astype(jnp.float32).reshape(sequence_length, kv_local, HEAD_SIZE).transpose(1, 0, 2)
    heads_of_norm = log_softmax_norm.reshape(kv_local, group_size, sequence_length)

    def per_head(head_inputs):
        query_one, grad_one, out_one, key_one, value_one, norm_one = head_inputs
        delta = jnp.sum(grad_one * out_one, axis=-1)
        scores = jnp.einsum("tgd,ud->gtu", query_one, key_one) * score_scale
        soft_probs = jnp.where(visible[None], jnp.exp(scores - norm_one[:, :, None]), 0.0)
        dprobs = jnp.einsum("tgd,ud->gtu", grad_one, value_one)
        dscores = low_round(soft_probs * (dprobs - delta.T[:, :, None]) * score_scale)
        probs_low = low_round(soft_probs)
        grad_query = jnp.einsum("gtu,ud->tgd", dscores, key_one)
        gradient_for_key = jnp.einsum("gtu,tgd->ud", dscores, query_one)
        gradient_for_value = jnp.einsum("gtu,tgd->ud", probs_low, grad_one)
        return grad_query, gradient_for_key, gradient_for_value

    grad_query, gradient_for_key, gradient_for_value = lax.map(
        per_head, (heads_of_queries, head_gradient, heads_of_output, heads_of_keys, heads_of_values, heads_of_norm))
    grad_q = grad_query.transpose(1, 0, 2, 3).reshape(sequence_length, -1).astype(jnp.bfloat16)
    key_gradient = gradient_for_key.transpose(1, 0, 2).reshape(sequence_length, -1).astype(jnp.bfloat16)
    value_gradient = gradient_for_value.transpose(1, 0, 2).reshape(sequence_length, -1).astype(jnp.bfloat16)
    return grad_q, key_gradient, value_gradient


def weight_for_sequence(inputs):
    features, key_rows = inputs
    local_width = key_rows.shape[-1]
    feature_blocks = features.astype(jnp.float32).reshape(N_CTX, BLOCK_TOKENS, DW)
    key_blocks = key_rows.astype(jnp.float32).reshape(HEAD_GROUPS, N_CTX, BLOCK_TOKENS, local_width)
    key_blocks = key_blocks.transpose(1, 2, 0, 3).reshape(N_CTX, BLOCK_TOKENS, HEAD_GROUPS * local_width)
    partials = jnp.einsum("cti,ctj->cij", feature_blocks, key_blocks)
    return jnp.sum(low_round(partials), axis=0)


def reference(block_pos, queries, keys, values, attention_output, output_gradient, log_softmax_norm, features):
    block_rows = jnp.repeat(block_pos, HEAD_GROUPS, axis=0)
    grad_q, key_gradient, value_gradient = lax.map(
        one_row, (block_rows, queries, keys, values, attention_output, output_gradient, log_softmax_norm))
    key_by_sequence = key_gradient.reshape(SEQUENCE_COUNT, HEAD_GROUPS, SEQUENCE_TOKENS, key_gradient.shape[-1])
    weight_parts = lax.map(weight_for_sequence, (features, key_by_sequence))
    return grad_q, key_gradient, value_gradient, jnp.sum(weight_parts, axis=0)
```

```python
import jax
import jax.numpy as jnp
from jax import lax
from jax.experimental import pallas as pl
from jax.experimental.pallas import tpu as pltpu
from jax.sharding import Mesh
from jax.sharding import PartitionSpec as P

HEADS = 5
HEAD_SIZE = 128
BLOCK = 128
WIDTH = HEADS * HEAD_SIZE
SIDE = 4
SCALE = HEAD_SIZE ** (-0.5)
CTX = ("x", "zh")
FSDP = ("zl", "y", "c")
Q_ROWS = 2 * BLOCK + 16
KV_ROWS = 2 * BLOCK + 16


def split_parts(value):
    parts = []
    for _ in range(3):
        part = lax.reduce_precision(value, 8, 7)
        parts.append(part.astype(jnp.bfloat16))
        value = value - part
    return parts


def dot(a, b, dims):
    return lax.dot_general(a, b, (dims, ((), ())), preferred_element_type=jnp.float32)


def attention_kernel(q_place, k_place, q_ref, kv_ref, dq_ref, dk_ref, dv_ref, dq_acc, dk_acc, dv_acc):
    dq_acc[...] = jnp.zeros_like(dq_acc)
    dk_acc[...] = jnp.zeros_like(dk_acc)
    dv_acc[...] = jnp.zeros_like(dv_acc)
    key_row = lax.broadcasted_iota(jnp.int32, (BLOCK, BLOCK), 0)
    query_col = lax.broadcasted_iota(jnp.int32, (BLOCK, BLOCK), 1)
    offset = key_row - query_col

    def pair(index, carry):
        j = index // SIDE
        i = index % SIDE
        ahead = (q_place[i] - k_place[j]) * BLOCK

        @pl.when(ahead >= 0)
        def _():
            k = kv_ref[j, :BLOCK, :]
            v = kv_ref[j, BLOCK : 2 * BLOCK, :]
            k_t = k.T
            rows = q_ref[i, 2 * BLOCK :, :].astype(jnp.float32)
            norm = rows[0:1] + rows[1:2] + rows[2:3]
            delta = rows[3:4] + rows[4:5] + rows[5:6]
            visible = offset <= ahead
            dk = dk_acc[j]
            dv = dv_acc[j]
            for h in range(HEADS):
                cols = slice(h * HEAD_SIZE, (h + 1) * HEAD_SIZE)
                q = q_ref[i, :BLOCK, cols]
                g = q_ref[i, BLOCK : 2 * BLOCK, cols]
                scores = dot(k, q, ((1,), (1,))) * SCALE
                probs = jnp.where(visible, jnp.exp(scores - norm[:, cols]), 0.0)
                dprobs = dot(v, g, ((1,), (1,)))
                dscores = (probs * (dprobs - delta[:, cols]) * SCALE).astype(jnp.bfloat16)
                dk = dk + dot(dscores, q, ((1,), (0,)))
                dv = dv + dot(probs.astype(jnp.bfloat16), g, ((1,), (0,)))
                dq_acc[i, :, cols] += dot(k_t, dscores, ((1,), (0,)))
            dk_acc[j] = dk
            dv_acc[j] = dv

        return carry

    lax.fori_loop(0, SIDE * SIDE, pair, 0)
    dq_ref[...] = dq_acc[...].astype(jnp.bfloat16)
    dk_ref[...] = dk_acc[...].astype(jnp.bfloat16)
    dv_ref[...] = dv_acc[...].astype(jnp.bfloat16)


def attention_grads(q_place, k_place, q_all, kv_all):
    smem = pl.BlockSpec(memory_space=pltpu.SMEM)
    vmem = pl.BlockSpec(memory_space=pltpu.VMEM)
    return pl.pallas_call(
        attention_kernel,
        out_shape=(
            jax.ShapeDtypeStruct((SIDE, HEAD_SIZE, WIDTH), jnp.bfloat16),
            jax.ShapeDtypeStruct((SIDE, BLOCK, HEAD_SIZE), jnp.bfloat16),
            jax.ShapeDtypeStruct((SIDE, BLOCK, HEAD_SIZE), jnp.bfloat16),
        ),
        in_specs=[smem, smem, vmem, vmem],
        out_specs=(vmem, vmem, vmem),
        scratch_shapes=[
            pltpu.VMEM((SIDE, HEAD_SIZE, WIDTH), jnp.float32),
            pltpu.VMEM((SIDE, BLOCK, HEAD_SIZE), jnp.float32),
            pltpu.VMEM((SIDE, BLOCK, HEAD_SIZE), jnp.float32),
        ],
        name="attention_grads",
    )(q_place, k_place, q_all, kv_all)


def share(value, axis):
    count = lax.axis_size(axis)
    return lax.all_to_all(
        jnp.broadcast_to(value[None], (count,) + value.shape), axis, 0, 0, tiled=True
    )


def swap_sum(value, axis):
    got = lax.all_to_all(value, axis, 0, 0, tiled=True)
    return jnp.sum(got.astype(jnp.float32), axis=0)


def local(block_pos, queries, keys, values, attention_output, output_gradient, log_softmax_norm, features):
    sequence = lax.axis_index("zl") * 2 + lax.axis_index("y") // 2
    place = lax.dynamic_slice_in_dim(block_pos, sequence, 1, 0)[0, 0].astype(jnp.bfloat16)
    gradient = output_gradient[0]
    product = gradient.astype(jnp.float32) * attention_output[0].astype(jnp.float32)
    delta = jnp.sum(product.reshape(BLOCK, HEADS, HEAD_SIZE), axis=-1).T.reshape(WIDTH)
    norm = log_softmax_norm[0].reshape(WIDTH)
    place_row = jnp.full((WIDTH,), place)
    extra = jnp.stack(split_parts(norm) + split_parts(delta) + [place_row] * 10)
    q_own = jnp.concatenate([queries[0], gradient, extra], axis=0)
    kv_own = jnp.concatenate(
        [keys[0], values[0], jnp.full((16, HEAD_SIZE), place)], axis=0
    )
    kv_all = share(kv_own, "zh")
    q_all = share(q_own, "x")
    q_place = q_all[:, 2 * BLOCK + 6, 0].astype(jnp.int32)
    k_place = kv_all[:, 2 * BLOCK, 0].astype(jnp.int32)
    dq, dk, dv = attention_grads(q_place, k_place, q_all, kv_all)

    key_gradient = swap_sum(dk, "zh").astype(jnp.bfloat16)
    grad_q = swap_sum(dq, "x")
    grad_q = grad_q.reshape(HEAD_SIZE, HEADS, BLOCK).transpose(2, 1, 0).reshape(BLOCK, WIDTH)
    value_gradient = swap_sum(dv, "zh").astype(jnp.bfloat16)

    gathered = share(key_gradient, "zl")
    gathered = share(gathered, "y")
    gathered = share(gathered, "c")
    gathered = gathered.reshape(2, 2, 2, 4, BLOCK, HEAD_SIZE)
    own = features.reshape(4, 2, BLOCK, features.shape[-1])
    partial = jnp.einsum("zhtf,chlztj->lcfj", own, gathered, preferred_element_type=jnp.float32)
    partial = partial.reshape(4, features.shape[-1], HEAD_SIZE)
    mine = swap_sum(partial.astype(jnp.bfloat16), "x")
    mine = jnp.sum(share(mine.astype(jnp.bfloat16), "zh").astype(jnp.float32), axis=0)
    grad_wk = share(mine, "x").transpose(1, 0, 2).reshape(features.shape[-1], 4 * HEAD_SIZE)
    return (grad_q.astype(jnp.bfloat16)[None], key_gradient[None], value_gradient[None], grad_wk)


def solution(mesh):
    fine = Mesh(mesh.devices.reshape(4, 4, 4, 4, 2), CTX + FSDP)
    return jax.shard_map(
        local,
        mesh=fine,
        in_specs=(
            P(None, CTX),
            P(FSDP, CTX, None),
            P(FSDP, CTX, None),
            P(FSDP, CTX, None),
            P(FSDP, CTX, None),
            P(FSDP, CTX, None),
            P(FSDP, None, CTX),
            P(None, CTX, FSDP),
        ),
        out_specs=(P(FSDP, CTX, None), P(FSDP, CTX, None), P(FSDP, CTX, None), P(FSDP, None)),
        check_vma=False,
    )
```

```python
import jax
import jax.numpy as jnp
from jax import lax
from jax.experimental import pallas as pl
from jax.experimental.pallas import tpu as pltpu
from jax.sharding import Mesh
from jax.sharding import PartitionSpec as P


HEADS = 5
HEAD_SIZE = 128
BLOCK = 128
STACK = HEADS * BLOCK
SIDE = 4
SCALE = HEAD_SIZE ** (-0.5)
CTX = ("x", "zh")
FSDP = ("zl", "yh", "yl", "c")
PIECE = 24
Q_ROWS = 2 * STACK + 32
KV_ROWS = 2 * BLOCK + 16


def dot(a, b, dims):
    return lax.dot_general(a, b, (dims, ((), ())), preferred_element_type=jnp.float32)


def parts_of(value):
    first = value.astype(jnp.bfloat16)
    value = value - first.astype(jnp.float32)
    second = value.astype(jnp.bfloat16)
    value = value - second.astype(jnp.float32)
    return [first.astype(jnp.float32), second.astype(jnp.float32), value]


def own_place(places):
    return places[lax.axis_index("zl") * 2 + lax.axis_index("yh"), 0]


def key_pack_kernel(places, k_ref, v_ref, out_ref):
    tail = jnp.full((16, HEAD_SIZE), own_place(places), jnp.int32)
    tail = tail.astype(jnp.float32).astype(jnp.bfloat16)
    for copy in range(SIDE):
        out_ref[copy, :BLOCK, :] = k_ref[0]
        out_ref[copy, BLOCK : 2 * BLOCK, :] = v_ref[0]
        out_ref[copy, 2 * BLOCK :, :] = tail


def query_pack_kernel(places, q_ref, g_ref, o_ref, norm_ref, out_ref):
    deltas = []
    for h in range(HEADS):
        cols = slice(h * HEAD_SIZE, (h + 1) * HEAD_SIZE)
        rows = slice(h * BLOCK, (h + 1) * BLOCK)
        out_ref[rows, :] = q_ref[0, :, cols]
        g = g_ref[0, :, cols]
        out_ref[STACK + h * BLOCK : STACK + (h + 1) * BLOCK, :] = g
        product = g.astype(jnp.float32) * o_ref[0, :, cols].astype(jnp.float32)
        deltas.append(jnp.sum(product.T, axis=0, keepdims=True))
    delta = jnp.concatenate(deltas, axis=0)
    tail = jnp.full((2, HEAD_SIZE), own_place(places), jnp.int32).astype(jnp.float32)
    extra = jnp.concatenate(parts_of(norm_ref[0]) + parts_of(delta) + [tail], axis=0)
    out_ref[2 * STACK :, :] = extra.astype(jnp.bfloat16)


def place_of(rows):
    return jnp.max(rows.astype(jnp.float32)).astype(jnp.int32)


def attention_kernel(
    q0, q1, q2, q3, kv_ref, dq0, dq1, dq2, dq3, dk_ref, dv_ref, dq_acc, dk_acc, dv_acc, k_t, k_place
):
    dk_acc[...] = jnp.zeros_like(dk_acc)
    dv_acc[...] = jnp.zeros_like(dv_acc)
    key_row = lax.broadcasted_iota(jnp.int32, (BLOCK, STACK), 0)
    query_col = lax.broadcasted_iota(jnp.int32, (BLOCK, STACK), 1) & (BLOCK - 1)
    offset = key_row - query_col
    for j in range(SIDE):
        k_t[j] = kv_ref[j, :BLOCK, :].T
        k_place[j] = place_of(kv_ref[j, 2 * BLOCK :, :])
    for q_ref, dq_ref in ((q0, dq0), (q1, dq1), (q2, dq2), (q3, dq3)):
        dq_acc[...] = jnp.zeros_like(dq_acc)
        extra = q_ref[2 * STACK :, :].astype(jnp.float32)
        norm = extra[0:5] + extra[5:10] + extra[10:15]
        delta = extra[15:20] + extra[20:25] + extra[25:30]
        norm = jnp.concatenate([norm[h : h + 1] for h in range(HEADS)], axis=1)
        delta = jnp.concatenate([delta[h : h + 1] for h in range(HEADS)], axis=1)
        here = place_of(q_ref[2 * STACK + 16 :, :][14:])

        def pair(j, carry):
            ahead = (here - k_place[j]) * BLOCK

            @pl.when(ahead >= 0)
            def _():
                q = q_ref[:STACK, :]
                g = q_ref[STACK : 2 * STACK, :]
                scores = dot(kv_ref[j, :BLOCK, :], q, ((1,), (1,))) * SCALE
                probs = jnp.where(offset <= ahead, jnp.exp(scores - norm), 0.0)
                dprobs = dot(kv_ref[j, BLOCK : 2 * BLOCK, :], g, ((1,), (1,)))
                dscores = (probs * (dprobs - delta) * SCALE).astype(jnp.bfloat16)
                dv_acc[j] += dot(probs.astype(jnp.bfloat16), g, ((1,), (0,)))
                dk_acc[j] += dot(dscores, q, ((1,), (0,)))
                dq_acc[...] += dot(k_t[j], dscores, ((1,), (0,)))

            return carry

        lax.fori_loop(0, SIDE, pair, 0)
        dq_ref[...] = dq_acc[...].astype(jnp.bfloat16)
    dk_ref[...] = dk_acc[...].astype(jnp.bfloat16)
    ring = lax.axis_index("zh")
    for j in range(SIDE):
        dv_ref[j] = dv_acc[(ring + j) % SIDE].astype(jnp.bfloat16)


SMEM = pl.BlockSpec(memory_space=pltpu.SMEM)
VMEM = pl.BlockSpec(memory_space=pltpu.VMEM)


def struct(shape, dtype=jnp.bfloat16):
    return jax.ShapeDtypeStruct(shape, dtype)


def pack_keys(places, keys, values):
    return pl.pallas_call(
        key_pack_kernel,
        out_shape=struct((SIDE, KV_ROWS, HEAD_SIZE)),
        in_specs=[SMEM, VMEM, VMEM],
        out_specs=VMEM,
        name="pack_keys",
    )(places, keys, values)


def pack_queries(places, queries, gradient, output, norm):
    return pl.pallas_call(
        query_pack_kernel,
        out_shape=struct((Q_ROWS, HEAD_SIZE)),
        in_specs=[SMEM] + [VMEM] * 4,
        out_specs=VMEM,
        name="pack_queries",
    )(places, queries, gradient, output, norm)


def attention_grads(q_parts, kv_all):
    return pl.pallas_call(
        attention_kernel,
        out_shape=(struct((HEAD_SIZE, STACK)),) * 4 + (struct((SIDE, BLOCK, HEAD_SIZE)),) * 2,
        in_specs=[VMEM] * 5,
        out_specs=(VMEM,) * 6,
        scratch_shapes=[
            pltpu.VMEM((HEAD_SIZE, STACK), jnp.float32),
            pltpu.VMEM((SIDE, BLOCK, HEAD_SIZE), jnp.float32),
            pltpu.VMEM((SIDE, BLOCK, HEAD_SIZE), jnp.float32),
            pltpu.VMEM((SIDE, HEAD_SIZE, BLOCK), jnp.bfloat16),
            pltpu.SMEM((SIDE,), jnp.int32),
        ],
        name="attention_grads",
    )(*q_parts, kv_all)


def ahead(value, axis, steps):
    count = lax.axis_size(axis)
    pairs = [(source, (source + steps) % count) for source in range(count)]
    return lax.ppermute(value, axis, pairs)


def swap(value, axis):
    return lax.all_to_all(value, axis, 0, 0, tiled=True)


def copies(value, count):
    return jnp.broadcast_to(value[None], (count,) + value.shape)


def total(parts):
    return jnp.sum(parts.astype(jnp.float32), axis=0)


def padded_features(features):
    ft = features.transpose(0, 2, 1)
    ft = ahead_pair(ft, "c")
    ft = ahead_pair(ft, "yl")
    rows = features.shape[-1] // SIDE
    ft = ft.reshape(SIDE, 8, SIDE, rows, BLOCK)
    ft = jnp.pad(ft, ((0, 0), (0, 0), (0, 0), (0, PIECE - rows), (0, 0)))
    return ft.transpose(1, 2, 0, 3, 4).reshape(8, SIDE * SIDE * PIECE, BLOCK)


def ahead_pair(value, axis):
    other = ahead(value, axis, 1)
    first = lax.axis_index(axis) == 0
    return jnp.stack([jnp.where(first, value, other), jnp.where(first, other, value)])


def whole(block_pos, queries, keys, values, attention_output, output_gradient, log_softmax_norm, features):
    kv_own = pack_keys(block_pos, keys, values)
    kv_all = swap(kv_own, "zh")
    q_own = pack_queries(block_pos, queries, output_gradient, attention_output, log_softmax_norm)
    q_parts = [q_own] + [ahead(q_own, "x", s) for s in (1, 2, 3)]
    *dq, dk, dv = attention_grads(q_parts, kv_all)

    key_gradient = total(swap(dk, "zh")).astype(jnp.bfloat16)
    dq = [dq[0]] + [ahead(dq[s], "x", -s) for s in (1, 2, 3)]
    grad_q = total(jnp.stack(dq))
    grad_q = grad_q.reshape(HEAD_SIZE, HEADS, BLOCK).transpose(2, 1, 0).reshape(BLOCK, STACK)
    dv = [dv[0]] + [ahead(dv[s], "zh", s) for s in (1, 2, 3)]
    value_gradient = total(jnp.stack(dv)).astype(jnp.bfloat16)

    weights = padded_features(features)
    gathered = swap(copies(key_gradient, 8), ("zl", "yh"))
    partial = jnp.einsum("smt,stj->mj", weights, gathered, preferred_element_type=jnp.float32)
    partial = partial.astype(jnp.bfloat16).reshape(SIDE, SIDE * PIECE, HEAD_SIZE)
    mine = total(swap(partial, "x"))
    mine = total(swap(copies(mine.astype(jnp.bfloat16), SIDE), "zh"))
    out = swap(copies(mine, SIDE).reshape(16, PIECE, HEAD_SIZE), ("x", "yl", "c"))
    width = features.shape[-1]
    out = out.reshape(SIDE, SIDE, PIECE, HEAD_SIZE)[:, :, : width // SIDE]
    grad_wk = out.transpose(0, 2, 1, 3).reshape(width, SIDE * HEAD_SIZE)
    return (grad_q.astype(jnp.bfloat16)[None], key_gradient[None], value_gradient[None], grad_wk)


def solution(mesh):
    fine = Mesh(mesh.devices.reshape(4, 4, 4, 2, 2, 2), CTX + FSDP)
    return jax.shard_map(
        whole,
        mesh=fine,
        in_specs=(
            P(None, CTX),
            P(FSDP, CTX, None),
            P(FSDP, CTX, None),
            P(FSDP, CTX, None),
            P(FSDP, CTX, None),
            P(FSDP, CTX, None),
            P(FSDP, None, CTX),
            P(None, CTX, FSDP),
        ),
        out_specs=(P(FSDP, CTX, None), P(FSDP, CTX, None), P(FSDP, CTX, None), P(FSDP, None)),
        check_vma=False,
    )
```

```python
import jax
import jax.numpy as jnp
from jax import lax
from jax.experimental import pallas as pl
from jax.experimental.pallas import tpu as pltpu
from jax.sharding import Mesh
from jax.sharding import PartitionSpec as P


HEADS = 5
HEAD_SIZE = 128
BLOCK = 128
STACK = HEADS * BLOCK
SIDE = 4
SCALE = HEAD_SIZE ** (-0.5)
LOG2E = 1.4426950408889634
CTX = ("x", "zh")
FSDP = ("zl", "yh", "yl", "c")
GRANT = 16 * 2**20
Q_ROWS = 2 * STACK + 32
KV_ROWS = 2 * BLOCK + 16


def dot(a, b, dims):
    return lax.dot_general(a, b, (dims, ((), ())), preferred_element_type=jnp.float32)


def parts_of(value):
    first = value.astype(jnp.bfloat16)
    value = value - first.astype(jnp.float32)
    second = value.astype(jnp.bfloat16)
    value = value - second.astype(jnp.float32)
    return [first.astype(jnp.float32), second.astype(jnp.float32), value]


def own_place(places):
    return places[0, lax.axis_index("zl") * 2 + lax.axis_index("yh")]


def pack_kernel(places, q_ref, g_ref, o_ref, norm_ref, k_ref, v_ref, q_out, kv_out):
    place = own_place(places)
    deltas = []
    for h in range(HEADS):
        cols = slice(h * HEAD_SIZE, (h + 1) * HEAD_SIZE)
        q = q_ref[0, :, cols]
        g = g_ref[0, :, cols]
        for copy in range(SIDE):
            q_out[copy, h * BLOCK : (h + 1) * BLOCK, :] = q
            q_out[copy, STACK + h * BLOCK : STACK + (h + 1) * BLOCK, :] = g
        product = g.astype(jnp.float32) * o_ref[0, :, cols].astype(jnp.float32)
        deltas.append(jnp.sum(product.T, axis=0, keepdims=True))
    delta = jnp.concatenate(deltas, axis=0)
    norm = norm_ref[:, 0, :] * LOG2E
    tail = jnp.full((2, HEAD_SIZE), place, jnp.int32).astype(jnp.float32)
    extra = jnp.concatenate(parts_of(norm) + parts_of(delta) + [tail], axis=0)
    for copy in range(SIDE):
        q_out[copy, 2 * STACK :, :] = extra.astype(jnp.bfloat16)
    kv_out[:BLOCK, :] = k_ref[0]
    kv_out[BLOCK : 2 * BLOCK, :] = v_ref[0]
    tail = jnp.full((16, HEAD_SIZE), place, jnp.int32)
    kv_out[2 * BLOCK :, :] = tail.astype(jnp.float32).astype(jnp.bfloat16)


def place_of(rows):
    return jnp.max(rows.astype(jnp.float32)).astype(jnp.int32)


def attention_kernel(q_all, kv_ref, dq_ref, dkv_ref, dq_acc, dk_acc, dv_acc, k_t, k_place):
    dk_acc[...] = jnp.zeros_like(dk_acc)
    dv_acc[...] = jnp.zeros_like(dv_acc)
    key_row = lax.broadcasted_iota(jnp.int32, (BLOCK, STACK), 0)
    query_col = lax.broadcasted_iota(jnp.int32, (BLOCK, STACK), 1) & (BLOCK - 1)
    offset = key_row - query_col
    for j in range(SIDE):
        k_t[j] = kv_ref[j, :BLOCK, :].T
        k_place[j] = place_of(kv_ref[j, 2 * BLOCK :, :])
    for i in range(SIDE):
        q_ref = q_all.at[i]
        dq_acc[...] = jnp.zeros_like(dq_acc)
        extra = q_ref[2 * STACK :, :].astype(jnp.float32)
        norm = extra[0:5] + extra[5:10] + extra[10:15]
        delta = extra[15:20] + extra[20:25] + extra[25:30]
        norm = jnp.concatenate([norm[h : h + 1] for h in range(HEADS)], axis=1)
        delta = jnp.concatenate([delta[h : h + 1] for h in range(HEADS)], axis=1)
        here = place_of(extra[30:32])

        def pair(j, carry):
            ahead = (here - k_place[j]) * BLOCK

            @pl.when(ahead >= 0)
            def _():
                q = q_ref[:STACK, :]
                g = q_ref[STACK : 2 * STACK, :]
                scores = dot(kv_ref[j, :BLOCK, :], q, ((1,), (1,))) * (SCALE * LOG2E)
                probs = jnp.where(offset <= ahead, jnp.exp2(scores - norm), 0.0)
                dprobs = dot(kv_ref[j, BLOCK : 2 * BLOCK, :], g, ((1,), (1,)))
                dscores = (probs * (dprobs - delta) * SCALE).astype(jnp.bfloat16)
                dv_acc[j] += dot(probs.astype(jnp.bfloat16), g, ((1,), (0,)))
                dk_acc[j] += dot(dscores, q, ((1,), (0,)))
                dq_acc[...] += dot(k_t[j], dscores, ((1,), (0,)))

            return carry

        lax.fori_loop(0, SIDE, pair, 0)
        dq_ref[i] = dq_acc[...].astype(jnp.bfloat16)
    dkv_ref[:, :BLOCK, :] = dk_acc[...].astype(jnp.bfloat16)
    dkv_ref[:, BLOCK:, :] = dv_acc[...].astype(jnp.bfloat16)


SMEM = pl.BlockSpec(memory_space=pltpu.SMEM)
VMEM = pl.BlockSpec(memory_space=pltpu.VMEM)


def struct(shape, dtype=jnp.bfloat16):
    return jax.ShapeDtypeStruct(shape, dtype)


def pack(places, queries, gradient, output, norm, keys, values):
    return pl.pallas_call(
        pack_kernel,
        out_shape=(struct((SIDE, Q_ROWS, HEAD_SIZE)), struct((KV_ROWS, HEAD_SIZE))),
        in_specs=[SMEM] + [VMEM] * 6,
        out_specs=(VMEM, VMEM),
        name="pack",
    )(places, queries, gradient, output, norm, keys, values)


def attention_grads(q_all, kv_all):
    return pl.pallas_call(
        attention_kernel,
        out_shape=(struct((SIDE, HEAD_SIZE, STACK)), struct((SIDE, 2 * BLOCK, HEAD_SIZE))),
        in_specs=[VMEM] * 2,
        out_specs=(VMEM,) * 2,
        scratch_shapes=[
            pltpu.VMEM((HEAD_SIZE, STACK), jnp.float32),
            pltpu.VMEM((SIDE, BLOCK, HEAD_SIZE), jnp.float32),
            pltpu.VMEM((SIDE, BLOCK, HEAD_SIZE), jnp.float32),
            pltpu.VMEM((SIDE, HEAD_SIZE, BLOCK), jnp.bfloat16),
            pltpu.SMEM((SIDE,), jnp.int32),
        ],
        compiler_params=pltpu.CompilerParams(vmem_limit_bytes=GRANT),
        name="attention_grads",
    )(q_all, kv_all)


def ahead(value, axis, steps):
    count = lax.axis_size(axis)
    pairs = [(source, (source + steps) % count) for source in range(count)]
    return lax.ppermute(value, axis, pairs)


def swap(value, axis):
    return lax.all_to_all(value, axis, 0, 0, tiled=True)


def copies(value, count):
    return jnp.broadcast_to(value[None], (count,) + value.shape)


def total(parts):
    return jnp.sum(parts.astype(jnp.float32), axis=0)


def row_features(features):
    rows = features.transpose(0, 2, 1)
    rows = ahead_pair(rows, "yl")
    rows = ahead_pair(rows, "c").transpose(1, 0, 2, 3, 4)
    return rows.reshape((SIDE,) + rows.shape[2:])


def ahead_pair(value, axis):
    other = ahead(value, axis, 1)
    first = lax.axis_index(axis) == 0
    return jnp.stack([jnp.where(first, value, other), jnp.where(first, other, value)])


def whole(block_pos, queries, keys, values, attention_output, output_gradient, log_softmax_norm, features):
    places = block_pos.T
    norm = log_softmax_norm.transpose(1, 0, 2)
    q_own, kv_own = pack(
        places, queries, output_gradient, attention_output, norm, keys, values
    )
    q_all = swap(q_own, "x")
    kv_all = lax.all_gather(kv_own, "zh", axis=0)
    dq, dkv = attention_grads(q_all, kv_all)

    dkv = swap(dkv, "zh")
    key_gradient = total(dkv[:, :BLOCK]).astype(jnp.bfloat16)
    value_gradient = total(dkv[:, BLOCK:]).astype(jnp.bfloat16)
    here = lax.axis_index("x")
    pieces = [lax.dynamic_index_in_dim(dq, (here + s) % SIDE, 0, keepdims=False) for s in range(SIDE)]
    dq = pieces[:1] + [ahead(pieces[s], "x", s) for s in (1, 2, 3)]
    grad_q = total(jnp.stack(dq))
    grad_q = grad_q.reshape(HEAD_SIZE, HEADS, BLOCK).transpose(2, 1, 0).reshape(BLOCK, STACK)

    weights = row_features(features)
    gathered = swap(copies(key_gradient, 8), ("zl", "yh"))
    partial = jnp.einsum("fsit,stj->fij", weights, gathered, preferred_element_type=jnp.float32)
    partial = copies(partial.astype(jnp.bfloat16), SIDE).reshape((16,) + partial.shape[1:])
    partial = swap(partial, ("x", "yl", "c"))
    mine = total(partial.reshape((SIDE, SIDE) + partial.shape[1:])).astype(jnp.bfloat16)
    mine = lax.all_gather(mine, "zh", axis=0)
    width = features.shape[-1]
    grad_wk = total(mine).transpose(1, 0, 2).reshape(width, SIDE * HEAD_SIZE)
    return (grad_q.astype(jnp.bfloat16)[None], key_gradient[None], value_gradient[None], grad_wk)


def solution(mesh):
    fine = Mesh(mesh.devices.reshape(4, 4, 4, 2, 2, 2), CTX + FSDP)
    return jax.shard_map(
        whole,
        mesh=fine,
        in_specs=(
            P(None, CTX),
            P(FSDP, CTX, None),
            P(FSDP, CTX, None),
            P(FSDP, CTX, None),
            P(FSDP, CTX, None),
            P(FSDP, CTX, None),
            P(FSDP, None, CTX),
            P(None, CTX, FSDP),
        ),
        out_specs=(P(FSDP, CTX, None), P(FSDP, CTX, None), P(FSDP, CTX, None), P(FSDP, None)),
        check_vma=False,
    )
```

```python
import jax
import jax.numpy as jnp
from jax import lax
from jax.experimental import pallas as pl
from jax.experimental.pallas import tpu as pltpu
from jax.sharding import Mesh
from jax.sharding import PartitionSpec as P


HEADS = 5
HEAD_SIZE = 128
BLOCK = 128
STACK = HEADS * BLOCK
SIDE = 4
SCALE = HEAD_SIZE ** (-0.5)
LOG2E = 1.4426950408889634
CTX = ("x", "zh")
FSDP = ("zl", "yh", "yl", "c")
GRANT = 16 * 2**20
Q_ROWS = 2 * STACK + 32
KV_ROWS = 2 * BLOCK + 16


def dot(a, b, dims):
    return lax.dot_general(a, b, (dims, ((), ())), preferred_element_type=jnp.float32)


def parts_of(value):
    first = value.astype(jnp.bfloat16)
    value = value - first.astype(jnp.float32)
    second = value.astype(jnp.bfloat16)
    value = value - second.astype(jnp.float32)
    return [first.astype(jnp.float32), second.astype(jnp.float32), value]


def own_place(places):
    return places[0, lax.axis_index("zl") * 2 + lax.axis_index("yh")]


def pack_kernel(places, q_ref, g_ref, o_ref, norm_ref, k_ref, v_ref, q_out, kv_out):
    place = own_place(places)
    deltas = []
    for h in range(HEADS):
        cols = slice(h * HEAD_SIZE, (h + 1) * HEAD_SIZE)
        q = q_ref[0, :, cols]
        g = g_ref[0, :, cols]
        for copy in range(SIDE):
            q_out[copy, h * BLOCK : (h + 1) * BLOCK, :] = q
            q_out[copy, STACK + h * BLOCK : STACK + (h + 1) * BLOCK, :] = g
        product = g.astype(jnp.float32) * o_ref[0, :, cols].astype(jnp.float32)
        deltas.append(jnp.sum(product.T, axis=0, keepdims=True))
    delta = jnp.concatenate(deltas, axis=0)
    norm = norm_ref[:, 0, :] * LOG2E
    tail = jnp.full((2, HEAD_SIZE), place, jnp.int32).astype(jnp.float32)
    extra = jnp.concatenate(parts_of(norm) + parts_of(delta) + [tail], axis=0)
    for copy in range(SIDE):
        q_out[copy, 2 * STACK :, :] = extra.astype(jnp.bfloat16)
    kv_out[:BLOCK, :] = k_ref[0]
    kv_out[BLOCK : 2 * BLOCK, :] = v_ref[0]
    tail = jnp.full((16, HEAD_SIZE), place, jnp.int32)
    kv_out[2 * BLOCK :, :] = tail.astype(jnp.float32).astype(jnp.bfloat16)


def place_of(rows):
    return jnp.max(rows.astype(jnp.float32)).astype(jnp.int32)


def attention_kernel(
    q_all, kv_ref, dq_ref, dkv_ref, k_s, v_s, k_t, dk_acc, dv_acc, rank, sorted_place
):
    dk_acc[...] = jnp.zeros_like(dk_acc)
    dv_acc[...] = jnp.zeros_like(dv_acc)
    key_row = lax.broadcasted_iota(jnp.int32, (BLOCK, STACK), 0)
    query_col = lax.broadcasted_iota(jnp.int32, (BLOCK, STACK), 1) & (BLOCK - 1)
    offset = key_row - query_col
    places = [place_of(kv_ref[j, 2 * BLOCK :, :]) for j in range(SIDE)]
    for j in range(SIDE):
        r = sum((places[m] < places[j]).astype(jnp.int32) for m in range(SIDE) if m != j)
        rank[j] = r
        sorted_place[r] = places[j]
        at = pl.multiple_of(r * BLOCK, BLOCK)
        k = kv_ref[j, :BLOCK, :]
        k_s[pl.ds(at, BLOCK), :] = k
        v_s[pl.ds(at, BLOCK), :] = kv_ref[j, BLOCK : 2 * BLOCK, :]
        k_t[r] = k.T

    def row(i, carry):
        q_ref = q_all.at[i]
        extra = q_ref[2 * STACK :, :].astype(jnp.float32)
        norm = extra[0:5] + extra[5:10] + extra[10:15]
        delta = extra[15:20] + extra[20:25] + extra[25:30]
        norm = jnp.concatenate([norm[h : h + 1] for h in range(HEADS)], axis=1)
        delta = jnp.concatenate([delta[h : h + 1] for h in range(HEADS)], axis=1)
        here = place_of(extra[30:32])
        seen = sum((sorted_place[j] <= here).astype(jnp.int32) for j in range(SIDE))

        @pl.when(seen == 0)
        def _():
            dq_ref[i] = jnp.zeros((HEAD_SIZE, STACK), jnp.bfloat16)

        for count in range(1, SIDE + 1):

            @pl.when(seen == count)
            def _(count=count):
                rows = count * BLOCK
                q = q_ref[:STACK, :]
                g = q_ref[STACK : 2 * STACK, :]
                last = (here - sorted_place[count - 1]) * BLOCK
                scores = dot(k_s[:rows, :], q, ((1,), (1,))) * (SCALE * LOG2E)
                probs = jnp.exp2(scores - norm)
                tail = jnp.where(offset <= last, probs[rows - BLOCK :], 0.0)
                probs = jnp.concatenate([probs[: rows - BLOCK], tail], axis=0) if count > 1 else tail
                dprobs = dot(v_s[:rows, :], g, ((1,), (1,)))
                dscores = (probs * (dprobs - delta) * SCALE).astype(jnp.bfloat16)
                dv_acc[:rows, :] += dot(probs.astype(jnp.bfloat16), g, ((1,), (0,)))
                dk_acc[:rows, :] += dot(dscores, q, ((1,), (0,)))
                k_cols = jnp.concatenate([k_t[j] for j in range(count)], axis=1)
                dq_ref[i] = dot(k_cols, dscores, ((1,), (0,))).astype(jnp.bfloat16)

        return carry

    lax.fori_loop(0, SIDE, row, 0)
    for j in range(SIDE):
        at = pl.multiple_of(rank[j] * BLOCK, BLOCK)
        dkv_ref[j, :BLOCK, :] = dk_acc[pl.ds(at, BLOCK), :].astype(jnp.bfloat16)
        dkv_ref[j, BLOCK:, :] = dv_acc[pl.ds(at, BLOCK), :].astype(jnp.bfloat16)


def fold_kernel(parts, copies_out, key_out, value_out):
    key = sum(parts[j, :BLOCK, :].astype(jnp.float32) for j in range(SIDE)).astype(jnp.bfloat16)
    for copy in range(8):
        copies_out[copy] = key
    key_out[0] = key
    value = sum(parts[j, BLOCK:, :].astype(jnp.float32) for j in range(SIDE))
    value_out[0] = value.astype(jnp.bfloat16)


def weight_kernel(rows, keys, out_ref):
    for f in range(SIDE):
        total = dot(rows[f, 0], keys[0], ((1,), (0,)))
        for s in range(1, 8):
            total += dot(rows[f, s], keys[s], ((1,), (0,)))
        total = total.astype(jnp.bfloat16)
        for copy in range(SIDE):
            out_ref[copy * SIDE + f] = total


SMEM = pl.BlockSpec(memory_space=pltpu.SMEM)
VMEM = pl.BlockSpec(memory_space=pltpu.VMEM)


def struct(shape, dtype=jnp.bfloat16):
    return jax.ShapeDtypeStruct(shape, dtype)


def pack(places, queries, gradient, output, norm, keys, values):
    return pl.pallas_call(
        pack_kernel,
        out_shape=(struct((SIDE, Q_ROWS, HEAD_SIZE)), struct((KV_ROWS, HEAD_SIZE))),
        in_specs=[SMEM] + [VMEM] * 6,
        out_specs=(VMEM, VMEM),
        name="pack",
    )(places, queries, gradient, output, norm, keys, values)


def attention_grads(q_all, kv_all):
    return pl.pallas_call(
        attention_kernel,
        out_shape=(struct((SIDE, HEAD_SIZE, STACK)), struct((SIDE, 2 * BLOCK, HEAD_SIZE))),
        in_specs=[VMEM] * 2,
        out_specs=(VMEM,) * 2,
        scratch_shapes=[
            pltpu.VMEM((SIDE * BLOCK, HEAD_SIZE), jnp.bfloat16),
            pltpu.VMEM((SIDE * BLOCK, HEAD_SIZE), jnp.bfloat16),
            pltpu.VMEM((SIDE, HEAD_SIZE, BLOCK), jnp.bfloat16),
            pltpu.VMEM((SIDE * BLOCK, HEAD_SIZE), jnp.float32),
            pltpu.VMEM((SIDE * BLOCK, HEAD_SIZE), jnp.float32),
            pltpu.SMEM((SIDE,), jnp.int32),
            pltpu.SMEM((SIDE,), jnp.int32),
        ],
        compiler_params=pltpu.CompilerParams(vmem_limit_bytes=GRANT),
        name="attention_grads",
    )(q_all, kv_all)


def fold(parts):
    block = (1, BLOCK, HEAD_SIZE)
    return pl.pallas_call(
        fold_kernel,
        out_shape=(struct((8, BLOCK, HEAD_SIZE)), struct(block), struct(block)),
        in_specs=[VMEM],
        out_specs=(VMEM,) * 3,
        compiler_params=pltpu.CompilerParams(vmem_limit_bytes=GRANT),
        name="fold",
    )(parts)


def weight_products(rows, keys):
    return pl.pallas_call(
        weight_kernel,
        out_shape=struct((SIDE * SIDE, rows.shape[2], HEAD_SIZE)),
        in_specs=[VMEM] * 2,
        out_specs=VMEM,
        compiler_params=pltpu.CompilerParams(vmem_limit_bytes=GRANT),
        name="weight_products",
    )(rows, keys)


def ahead(value, axis, steps):
    count = lax.axis_size(axis)
    pairs = [(source, (source + steps) % count) for source in range(count)]
    return lax.ppermute(value, axis, pairs)


def swap(value, axis):
    return lax.all_to_all(value, axis, 0, 0, tiled=True)


def total(parts):
    return jnp.sum(parts.astype(jnp.float32), axis=0)


def row_features(features):
    rows = features.transpose(0, 2, 1)
    rows = ahead_pair(rows, "yl")
    rows = ahead_pair(rows, "c").transpose(1, 0, 2, 3, 4)
    return rows.reshape((SIDE,) + rows.shape[2:])


def ahead_pair(value, axis):
    other = ahead(value, axis, 1)
    first = lax.axis_index(axis) == 0
    return jnp.stack([jnp.where(first, value, other), jnp.where(first, other, value)])


def whole(block_pos, queries, keys, values, attention_output, output_gradient, log_softmax_norm, features):
    places = block_pos.T
    norm = log_softmax_norm.transpose(1, 0, 2)
    q_own, kv_own = pack(
        places, queries, output_gradient, attention_output, norm, keys, values
    )
    q_all = swap(q_own, "x")
    kv_all = lax.all_gather(kv_own, "zh", axis=0)
    dq, dkv = attention_grads(q_all, kv_all)

    dkv = swap(dkv, "zh")
    key_copies, key_gradient, value_gradient = fold(dkv)
    here = lax.axis_index("x")
    pieces = [lax.dynamic_index_in_dim(dq, (here + s) % SIDE, 0, keepdims=False) for s in range(SIDE)]
    dq = pieces[:1] + [ahead(pieces[s], "x", s) for s in (1, 2, 3)]
    grad_q = total(jnp.stack(dq))
    grad_q = grad_q.reshape(HEAD_SIZE, HEADS, BLOCK).transpose(2, 1, 0).reshape(BLOCK, STACK)

    weights = row_features(features)
    gathered = swap(key_copies, ("zl", "yh"))
    partial = weight_products(weights, gathered)
    partial = swap(partial, ("x", "yl", "c"))
    mine = total(partial.reshape((SIDE, SIDE) + partial.shape[1:])).astype(jnp.bfloat16)
    mine = lax.all_gather(mine, "zh", axis=0)
    width = features.shape[-1]
    grad_wk = total(mine).transpose(1, 0, 2).reshape(width, SIDE * HEAD_SIZE)
    return (grad_q.astype(jnp.bfloat16)[None], key_gradient, value_gradient, grad_wk)


def solution(mesh):
    fine = Mesh(mesh.devices.reshape(4, 4, 4, 2, 2, 2), CTX + FSDP)
    return jax.shard_map(
        whole,
        mesh=fine,
        in_specs=(
            P(None, CTX),
            P(FSDP, CTX, None),
            P(FSDP, CTX, None),
            P(FSDP, CTX, None),
            P(FSDP, CTX, None),
            P(FSDP, CTX, None),
            P(FSDP, None, CTX),
            P(None, CTX, FSDP),
        ),
        out_specs=(P(FSDP, CTX, None), P(FSDP, CTX, None), P(FSDP, CTX, None), P(FSDP, None)),
        check_vma=False,
    )
```

```python
import jax
import jax.numpy as jnp
from jax import lax
from jax.experimental import pallas as pl
from jax.experimental.pallas import tpu as pltpu
from jax.sharding import Mesh
from jax.sharding import PartitionSpec as P


HEADS = 5
HEAD_SIZE = 128
BLOCK = 128
STACK = HEADS * BLOCK
SIDE = 4
SCALE = HEAD_SIZE ** (-0.5)
LOG2E = 1.4426950408889634
CTX = ("x", "zh")
FSDP = ("zl", "yh", "yl", "c")
GRANT = 16 * 2**20
Q_ROWS = 2 * STACK + 32
KV_ROWS = 2 * BLOCK + 16


def dot(a, b, dims):
    return lax.dot_general(a, b, (dims, ((), ())), preferred_element_type=jnp.float32)


def parts_of(value):
    first = value.astype(jnp.bfloat16)
    value = value - first.astype(jnp.float32)
    second = value.astype(jnp.bfloat16)
    value = value - second.astype(jnp.float32)
    return [first.astype(jnp.float32), second.astype(jnp.float32), value]


def own_place(places):
    return places[0, lax.axis_index("zl") * 2 + lax.axis_index("yh")]


def pack_kernel(places, q_ref, g_ref, o_ref, norm_ref, k_ref, v_ref, q_out, kv_out):
    place = own_place(places)
    deltas = []
    for h in range(HEADS):
        cols = slice(h * HEAD_SIZE, (h + 1) * HEAD_SIZE)
        q = q_ref[0, :, cols]
        g = g_ref[0, :, cols]
        for copy in range(SIDE):
            q_out[copy, h * BLOCK : (h + 1) * BLOCK, :] = q
            q_out[copy, STACK + h * BLOCK : STACK + (h + 1) * BLOCK, :] = g
        product = g.astype(jnp.float32) * o_ref[0, :, cols].astype(jnp.float32)
        deltas.append(jnp.sum(product.T, axis=0, keepdims=True))
    delta = jnp.concatenate(deltas, axis=0)
    norm = norm_ref[:, 0, :] * LOG2E
    tail = jnp.full((2, HEAD_SIZE), place, jnp.int32).astype(jnp.float32)
    extra = jnp.concatenate(parts_of(norm) + parts_of(delta) + [tail], axis=0)
    for copy in range(SIDE):
        q_out[copy, 2 * STACK :, :] = extra.astype(jnp.bfloat16)
    kv_out[:BLOCK, :] = k_ref[0]
    kv_out[BLOCK : 2 * BLOCK, :] = v_ref[0]
    tail = jnp.full((16, HEAD_SIZE), place, jnp.int32)
    kv_out[2 * BLOCK :, :] = tail.astype(jnp.float32).astype(jnp.bfloat16)


def places_of(blocks):
    digits = sum(rows.astype(jnp.float32) * 16.0**j for j, rows in enumerate(blocks))
    word = jnp.max(digits).astype(jnp.int32)
    return [(word >> (4 * j)) & 15 for j in range(len(blocks))]


def attention_kernel(
    q_all, kv_ref, dq_ref, dkv_ref, k_s, v_s, k_t, dk_acc, dv_acc, rank, sorted_place, q_place
):
    dk_acc[...] = jnp.zeros_like(dk_acc)
    dv_acc[...] = jnp.zeros_like(dv_acc)
    key_row = lax.broadcasted_iota(jnp.int32, (BLOCK, STACK), 0)
    query_col = lax.broadcasted_iota(jnp.int32, (BLOCK, STACK), 1) & (BLOCK - 1)
    offset = key_row - query_col
    places = places_of([kv_ref[j, 2 * BLOCK :, :] for j in range(SIDE)])
    tails = [q_all[i, 2 * STACK + 16 :, :].astype(jnp.float32)[14:] for i in range(SIDE)]
    for i, place in enumerate(places_of(tails)):
        q_place[i] = place
    for j in range(SIDE):
        r = sum((places[m] < places[j]).astype(jnp.int32) for m in range(SIDE) if m != j)
        rank[j] = r
        sorted_place[r] = places[j]
        at = pl.multiple_of(r * BLOCK, BLOCK)
        k = kv_ref[j, :BLOCK, :]
        k_s[pl.ds(at, BLOCK), :] = k
        v_s[pl.ds(at, BLOCK), :] = kv_ref[j, BLOCK : 2 * BLOCK, :]
        k_t[r] = k.T

    def row(i, carry):
        q_ref = q_all.at[i]
        extra = q_ref[2 * STACK :, :].astype(jnp.float32)
        norm = extra[0:5] + extra[5:10] + extra[10:15]
        delta = extra[15:20] + extra[20:25] + extra[25:30]
        norm = jnp.concatenate([norm[h : h + 1] for h in range(HEADS)], axis=1)
        delta = jnp.concatenate([delta[h : h + 1] for h in range(HEADS)], axis=1)
        here = q_place[i]
        seen = sum((sorted_place[j] <= here).astype(jnp.int32) for j in range(SIDE))

        @pl.when(seen == 0)
        def _():
            dq_ref[i] = jnp.zeros((HEAD_SIZE, STACK), jnp.bfloat16)

        for count in range(1, SIDE + 1):

            @pl.when(seen == count)
            def _(count=count):
                rows = count * BLOCK
                q = q_ref[:STACK, :]
                g = q_ref[STACK : 2 * STACK, :]
                last = (here - sorted_place[count - 1]) * BLOCK
                scores = dot(k_s[:rows, :], q, ((1,), (1,))) * (SCALE * LOG2E)
                probs = jnp.exp2(scores - norm)
                tail = jnp.where(offset <= last, probs[rows - BLOCK :], 0.0)
                probs = jnp.concatenate([probs[: rows - BLOCK], tail], axis=0) if count > 1 else tail
                dprobs = dot(v_s[:rows, :], g, ((1,), (1,)))
                dscores = (probs * (dprobs - delta) * SCALE).astype(jnp.bfloat16)
                dv_acc[:rows, :] += dot(probs.astype(jnp.bfloat16), g, ((1,), (0,)))
                dk_acc[:rows, :] += dot(dscores, q, ((1,), (0,)))
                k_cols = jnp.concatenate([k_t[j] for j in range(count)], axis=1)
                dq_ref[i] = dot(k_cols, dscores, ((1,), (0,))).astype(jnp.bfloat16)

        return carry

    lax.fori_loop(0, SIDE, row, 0)
    for j in range(SIDE):
        at = pl.multiple_of(rank[j] * BLOCK, BLOCK)
        dkv_ref[j, :BLOCK, :] = dk_acc[pl.ds(at, BLOCK), :].astype(jnp.bfloat16)
        dkv_ref[j, BLOCK:, :] = dv_acc[pl.ds(at, BLOCK), :].astype(jnp.bfloat16)


def fold_kernel(parts, copies_out, key_out, value_out):
    key = sum(parts[j, :BLOCK, :].astype(jnp.float32) for j in range(SIDE)).astype(jnp.bfloat16)
    for copy in range(8):
        copies_out[copy] = key
    key_out[0] = key
    value = sum(parts[j, BLOCK:, :].astype(jnp.float32) for j in range(SIDE))
    value_out[0] = value.astype(jnp.bfloat16)


def weight_kernel(rows, keys, out_ref):
    keys = keys[...].reshape(8 * BLOCK, HEAD_SIZE)
    for f in range(SIDE):
        left = jnp.concatenate([rows[f, s] for s in range(8)], axis=1)
        total = dot(left, keys, ((1,), (0,))).astype(jnp.bfloat16)
        for copy in range(SIDE):
            out_ref[copy * SIDE + f] = total


def finish_kernel(parts, d0, d1, d2, d3, wk_out, q_out):
    for r in range(SIDE):
        total = sum(parts[b * SIDE + r].astype(jnp.float32) for b in range(SIDE))
        wk_out[:, r * HEAD_SIZE : (r + 1) * HEAD_SIZE] = total
    for h in range(HEADS):
        cols = slice(h * HEAD_SIZE, (h + 1) * HEAD_SIZE)
        total = sum(d[:, cols].astype(jnp.float32) for d in (d0, d1, d2, d3))
        q_out[0, :, cols] = total.T.astype(jnp.bfloat16)


SMEM = pl.BlockSpec(memory_space=pltpu.SMEM)
VMEM = pl.BlockSpec(memory_space=pltpu.VMEM)


def struct(shape, dtype=jnp.bfloat16):
    return jax.ShapeDtypeStruct(shape, dtype)


def pack(places, queries, gradient, output, norm, keys, values):
    return pl.pallas_call(
        pack_kernel,
        out_shape=(struct((SIDE, Q_ROWS, HEAD_SIZE)), struct((KV_ROWS, HEAD_SIZE))),
        in_specs=[SMEM] + [VMEM] * 6,
        out_specs=(VMEM, VMEM),
        name="pack",
    )(places, queries, gradient, output, norm, keys, values)


def attention_grads(q_all, kv_all):
    return pl.pallas_call(
        attention_kernel,
        out_shape=(struct((SIDE, HEAD_SIZE, STACK)), struct((SIDE, 2 * BLOCK, HEAD_SIZE))),
        in_specs=[VMEM] * 2,
        out_specs=(VMEM,) * 2,
        scratch_shapes=[
            pltpu.VMEM((SIDE * BLOCK, HEAD_SIZE), jnp.bfloat16),
            pltpu.VMEM((SIDE * BLOCK, HEAD_SIZE), jnp.bfloat16),
            pltpu.VMEM((SIDE, HEAD_SIZE, BLOCK), jnp.bfloat16),
            pltpu.VMEM((SIDE * BLOCK, HEAD_SIZE), jnp.float32),
            pltpu.VMEM((SIDE * BLOCK, HEAD_SIZE), jnp.float32),
            pltpu.SMEM((SIDE,), jnp.int32),
            pltpu.SMEM((SIDE,), jnp.int32),
            pltpu.SMEM((SIDE,), jnp.int32),
        ],
        compiler_params=pltpu.CompilerParams(vmem_limit_bytes=GRANT),
        name="attention_grads",
    )(q_all, kv_all)


def fold(parts):
    block = (1, BLOCK, HEAD_SIZE)
    return pl.pallas_call(
        fold_kernel,
        out_shape=(struct((8, BLOCK, HEAD_SIZE)), struct(block), struct(block)),
        in_specs=[VMEM],
        out_specs=(VMEM,) * 3,
        compiler_params=pltpu.CompilerParams(vmem_limit_bytes=GRANT),
        name="fold",
    )(parts)


def weight_products(rows, keys):
    return pl.pallas_call(
        weight_kernel,
        out_shape=struct((SIDE * SIDE, rows.shape[2], HEAD_SIZE)),
        in_specs=[VMEM] * 2,
        out_specs=VMEM,
        compiler_params=pltpu.CompilerParams(vmem_limit_bytes=GRANT),
        name="weight_products",
    )(rows, keys)


def finish(parts, dq):
    width = parts.shape[1]
    return pl.pallas_call(
        finish_kernel,
        out_shape=(
            struct((width, SIDE * HEAD_SIZE), jnp.float32),
            struct((1, BLOCK, STACK)),
        ),
        in_specs=[VMEM] * 5,
        out_specs=(VMEM,) * 2,
        compiler_params=pltpu.CompilerParams(vmem_limit_bytes=GRANT),
        name="finish",
    )(parts, *dq)


def ahead(value, axis, steps):
    count = lax.axis_size(axis)
    pairs = [(source, (source + steps) % count) for source in range(count)]
    return lax.ppermute(value, axis, pairs)


def swap(value, axis):
    return lax.all_to_all(value, axis, 0, 0, tiled=True)


def total(parts):
    return jnp.sum(parts.astype(jnp.float32), axis=0)


def row_features(features):
    rows = features.transpose(0, 2, 1)
    rows = ahead_pair(rows, "yl")
    rows = ahead_pair(rows, "c").transpose(1, 0, 2, 3, 4)
    return rows.reshape((SIDE,) + rows.shape[2:])


def ahead_pair(value, axis):
    other = ahead(value, axis, 1)
    first = lax.axis_index(axis) == 0
    return jnp.stack([jnp.where(first, value, other), jnp.where(first, other, value)])


def whole(block_pos, queries, keys, values, attention_output, output_gradient, log_softmax_norm, features):
    places = block_pos.T
    norm = log_softmax_norm.transpose(1, 0, 2)
    q_own, kv_own = pack(
        places, queries, output_gradient, attention_output, norm, keys, values
    )
    q_all = swap(q_own, "x")
    kv_all = lax.all_gather(kv_own, "zh", axis=0)
    dq, dkv = attention_grads(q_all, kv_all)

    dkv = swap(dkv, "zh")
    key_copies, key_gradient, value_gradient = fold(dkv)
    here = lax.axis_index("x")
    pieces = [lax.dynamic_index_in_dim(dq, (here + s) % SIDE, 0, keepdims=False) for s in range(SIDE)]
    dq = pieces[:1] + [ahead(pieces[s], "x", s) for s in (1, 2, 3)]
    weights = row_features(features)
    gathered = swap(key_copies, ("zl", "yh"))
    partial = weight_products(weights, gathered)
    partial = swap(partial, ("x", "yl", "c"))
    mine = total(partial.reshape((SIDE, SIDE) + partial.shape[1:])).astype(jnp.bfloat16)
    mine = mine.reshape(SIDE, features.shape[-1], HEAD_SIZE)
    mine = lax.all_gather(mine, "zh", axis=0, tiled=True)
    grad_wk, grad_q = finish(mine, dq)
    return (grad_q, key_gradient, value_gradient, grad_wk)


def solution(mesh):
    fine = Mesh(mesh.devices.reshape(4, 4, 4, 2, 2, 2), CTX + FSDP)
    return jax.shard_map(
        whole,
        mesh=fine,
        in_specs=(
            P(None, CTX),
            P(FSDP, CTX, None),
            P(FSDP, CTX, None),
            P(FSDP, CTX, None),
            P(FSDP, CTX, None),
            P(FSDP, CTX, None),
            P(FSDP, None, CTX),
            P(None, CTX, FSDP),
        ),
        out_specs=(P(FSDP, CTX, None), P(FSDP, CTX, None), P(FSDP, CTX, None), P(FSDP, None)),
        check_vma=False,
    )
```

```python
import jax
import jax.numpy as jnp
from jax import lax
from jax.experimental import pallas as pl
from jax.experimental.pallas import tpu as pltpu
from jax.sharding import Mesh
from jax.sharding import PartitionSpec as P


HEADS = 5
HEAD_SIZE = 128
BLOCK = 128
STACK = HEADS * BLOCK
SIDE = 4
SCALE = HEAD_SIZE ** (-0.5)
LOG2E = 1.4426950408889634
CTX = ("x", "zh")
FSDP = ("s", "yl", "c")
GRANT = 16 * 2**20
Z_ORDER = (1, 0, 3, 2)
S_ORDER = (4, 5, 2, 3, 6, 7, 0, 1)
Q_ROWS = 2 * STACK + 32
KV_ROWS = 2 * BLOCK + 16


def dot(a, b, dims):
    return lax.dot_general(a, b, (dims, ((), ())), preferred_element_type=jnp.float32)


def parts_of(value):
    first = value.astype(jnp.bfloat16)
    value = value - first.astype(jnp.float32)
    second = value.astype(jnp.bfloat16)
    value = value - second.astype(jnp.float32)
    return [first.astype(jnp.float32), second.astype(jnp.float32), value]


def own_place(places):
    return places[0, lax.axis_index("s")]


def pack_kernel(places, q_ref, g_ref, o_ref, norm_ref, k_ref, v_ref, q_out, kv_out):
    place = own_place(places)
    deltas = []
    for h in range(HEADS):
        cols = slice(h * HEAD_SIZE, (h + 1) * HEAD_SIZE)
        q = q_ref[0, :, cols]
        g = g_ref[0, :, cols]
        for copy in range(SIDE):
            q_out[copy, h * BLOCK : (h + 1) * BLOCK, :] = q
            q_out[copy, STACK + h * BLOCK : STACK + (h + 1) * BLOCK, :] = g
        product = g.astype(jnp.float32) * o_ref[0, :, cols].astype(jnp.float32)
        deltas.append(jnp.sum(product.T, axis=0, keepdims=True))
    delta = jnp.concatenate(deltas, axis=0)
    norm = norm_ref[:, 0, :] * LOG2E
    tail = jnp.full((2, HEAD_SIZE), place, jnp.int32).astype(jnp.float32)
    extra = jnp.concatenate(parts_of(norm) + parts_of(delta) + [tail], axis=0)
    for copy in range(SIDE):
        q_out[copy, 2 * STACK :, :] = extra.astype(jnp.bfloat16)
    kv_out[:BLOCK, :] = k_ref[0]
    kv_out[BLOCK : 2 * BLOCK, :] = v_ref[0]
    tail = jnp.full((16, HEAD_SIZE), place, jnp.int32)
    kv_out[2 * BLOCK :, :] = tail.astype(jnp.float32).astype(jnp.bfloat16)


def places_of(blocks):
    digits = sum(rows.astype(jnp.float32) * 16.0**j for j, rows in enumerate(blocks))
    word = jnp.max(digits).astype(jnp.int32)
    return [(word >> (4 * j)) & 15 for j in range(len(blocks))]


def attention_kernel(
    q_all, kv_ref, dq_ref, dkv_ref, k_s, v_s, k_t, dk_acc, dv_acc, rank, sorted_place, q_place
):
    dk_acc[...] = jnp.zeros_like(dk_acc)
    dv_acc[...] = jnp.zeros_like(dv_acc)
    key_row = lax.broadcasted_iota(jnp.int32, (BLOCK, STACK), 0)
    query_col = lax.broadcasted_iota(jnp.int32, (BLOCK, STACK), 1) & (BLOCK - 1)
    offset = key_row - query_col
    places = places_of([kv_ref[j, 2 * BLOCK :, :] for j in range(SIDE)])
    tails = [q_all[i, 2 * STACK + 16 :, :].astype(jnp.float32)[14:] for i in range(SIDE)]
    for i, place in enumerate(places_of(tails)):
        q_place[i] = place
    for j in range(SIDE):
        r = sum((places[m] < places[j]).astype(jnp.int32) for m in range(SIDE) if m != j)
        rank[j] = r
        sorted_place[r] = places[j]
        at = pl.multiple_of(r * BLOCK, BLOCK)
        k = kv_ref[j, :BLOCK, :]
        k_s[pl.ds(at, BLOCK), :] = k
        v_s[pl.ds(at, BLOCK), :] = kv_ref[j, BLOCK : 2 * BLOCK, :]
        k_t[r] = k.T

    def row(i, carry):
        q_ref = q_all.at[i]
        extra = q_ref[2 * STACK :, :].astype(jnp.float32)
        norm = extra[0:5] + extra[5:10] + extra[10:15]
        delta = extra[15:20] + extra[20:25] + extra[25:30]
        norm = jnp.concatenate([norm[h : h + 1] for h in range(HEADS)], axis=1)
        delta = jnp.concatenate([delta[h : h + 1] for h in range(HEADS)], axis=1)
        here = q_place[i]
        seen = sum((sorted_place[j] <= here).astype(jnp.int32) for j in range(SIDE))

        @pl.when(seen == 0)
        def _():
            dq_ref[i] = jnp.zeros((HEAD_SIZE, STACK), jnp.bfloat16)

        for count in range(1, SIDE + 1):

            @pl.when(seen == count)
            def _(count=count):
                rows = count * BLOCK
                q = q_ref[:STACK, :]
                g = q_ref[STACK : 2 * STACK, :]
                last = (here - sorted_place[count - 1]) * BLOCK
                scores = dot(k_s[:rows, :], q, ((1,), (1,))) * (SCALE * LOG2E)
                probs = jnp.exp2(scores - norm)
                tail = jnp.where(offset <= last, probs[rows - BLOCK :], 0.0)
                probs = jnp.concatenate([probs[: rows - BLOCK], tail], axis=0) if count > 1 else tail
                dprobs = dot(v_s[:rows, :], g, ((1,), (1,)))
                dscores = (probs * (dprobs - delta) * SCALE).astype(jnp.bfloat16)
                dv_acc[:rows, :] += dot(probs.astype(jnp.bfloat16), g, ((1,), (0,)))
                dk_acc[:rows, :] += dot(dscores, q, ((1,), (0,)))
                k_cols = jnp.concatenate([k_t[j] for j in range(count)], axis=1)
                dq_ref[i] = dot(k_cols, dscores, ((1,), (0,))).astype(jnp.bfloat16)

        return carry

    lax.fori_loop(0, SIDE, row, 0)
    for j in range(SIDE):
        at = pl.multiple_of(rank[j] * BLOCK, BLOCK)
        slot = Z_ORDER.index(j)
        dkv_ref[slot, :BLOCK, :] = dk_acc[pl.ds(at, BLOCK), :].astype(jnp.bfloat16)
        dkv_ref[slot, BLOCK:, :] = dv_acc[pl.ds(at, BLOCK), :].astype(jnp.bfloat16)


def fold_kernel(parts, copies_out, key_out, value_out):
    key = sum(parts[j, :BLOCK, :].astype(jnp.float32) for j in range(SIDE)).astype(jnp.bfloat16)
    for copy in range(8):
        copies_out[copy] = key
    key_out[0] = key
    value = sum(parts[j, BLOCK:, :].astype(jnp.float32) for j in range(SIDE))
    value_out[0] = value.astype(jnp.bfloat16)


def weight_kernel(rows, keys, out_ref):
    keys = keys[...].reshape(8 * BLOCK, HEAD_SIZE)
    for f in range(SIDE):
        left = jnp.concatenate([rows[f, s] for s in S_ORDER], axis=1)
        total = dot(left, keys, ((1,), (0,))).astype(jnp.bfloat16)
        for copy in range(SIDE):
            out_ref[copy * SIDE + f] = total


def finish_kernel(parts, d0, d1, d2, d3, wk_out, q_out):
    for r in range(SIDE):
        total = sum(parts[b * SIDE + r].astype(jnp.float32) for b in range(SIDE))
        wk_out[:, r * HEAD_SIZE : (r + 1) * HEAD_SIZE] = total
    for h in range(HEADS):
        cols = slice(h * HEAD_SIZE, (h + 1) * HEAD_SIZE)
        total = sum(d[:, cols].astype(jnp.float32) for d in (d0, d1, d2, d3))
        q_out[0, :, cols] = total.T.astype(jnp.bfloat16)


SMEM = pl.BlockSpec(memory_space=pltpu.SMEM)
VMEM = pl.BlockSpec(memory_space=pltpu.VMEM)


def struct(shape, dtype=jnp.bfloat16):
    return jax.ShapeDtypeStruct(shape, dtype)


def pack(places, queries, gradient, output, norm, keys, values):
    return pl.pallas_call(
        pack_kernel,
        out_shape=(struct((SIDE, Q_ROWS, HEAD_SIZE)), struct((KV_ROWS, HEAD_SIZE))),
        in_specs=[SMEM] + [VMEM] * 6,
        out_specs=(VMEM, VMEM),
        name="pack",
    )(places, queries, gradient, output, norm, keys, values)


def attention_grads(q_all, kv_all):
    return pl.pallas_call(
        attention_kernel,
        out_shape=(struct((SIDE, HEAD_SIZE, STACK)), struct((SIDE, 2 * BLOCK, HEAD_SIZE))),
        in_specs=[VMEM] * 2,
        out_specs=(VMEM,) * 2,
        scratch_shapes=[
            pltpu.VMEM((SIDE * BLOCK, HEAD_SIZE), jnp.bfloat16),
            pltpu.VMEM((SIDE * BLOCK, HEAD_SIZE), jnp.bfloat16),
            pltpu.VMEM((SIDE, HEAD_SIZE, BLOCK), jnp.bfloat16),
            pltpu.VMEM((SIDE * BLOCK, HEAD_SIZE), jnp.float32),
            pltpu.VMEM((SIDE * BLOCK, HEAD_SIZE), jnp.float32),
            pltpu.SMEM((SIDE,), jnp.int32),
            pltpu.SMEM((SIDE,), jnp.int32),
            pltpu.SMEM((SIDE,), jnp.int32),
        ],
        compiler_params=pltpu.CompilerParams(vmem_limit_bytes=GRANT),
        name="attention_grads",
    )(q_all, kv_all)


def fold(parts):
    block = (1, BLOCK, HEAD_SIZE)
    return pl.pallas_call(
        fold_kernel,
        out_shape=(struct((8, BLOCK, HEAD_SIZE)), struct(block), struct(block)),
        in_specs=[VMEM],
        out_specs=(VMEM,) * 3,
        compiler_params=pltpu.CompilerParams(vmem_limit_bytes=GRANT),
        name="fold",
    )(parts)


def weight_products(rows, keys):
    return pl.pallas_call(
        weight_kernel,
        out_shape=struct((SIDE * SIDE, rows.shape[2], HEAD_SIZE)),
        in_specs=[VMEM] * 2,
        out_specs=VMEM,
        compiler_params=pltpu.CompilerParams(vmem_limit_bytes=GRANT),
        name="weight_products",
    )(rows, keys)


def finish(parts, dq):
    width = parts.shape[1]
    return pl.pallas_call(
        finish_kernel,
        out_shape=(
            struct((width, SIDE * HEAD_SIZE), jnp.float32),
            struct((1, BLOCK, STACK)),
        ),
        in_specs=[VMEM] * 5,
        out_specs=(VMEM,) * 2,
        compiler_params=pltpu.CompilerParams(vmem_limit_bytes=GRANT),
        name="finish",
    )(parts, *dq)


def ahead(value, axis, steps):
    count = lax.axis_size(axis)
    pairs = [(source, (source + steps) % count) for source in range(count)]
    return lax.ppermute(value, axis, pairs)


def swap(value, axis):
    return lax.all_to_all(value, axis, 0, 0, tiled=True)


def total(parts):
    return jnp.sum(parts.astype(jnp.float32), axis=0)


def row_features(features):
    rows = features.transpose(0, 2, 1)
    rows = ahead_pair(rows, "yl")
    rows = ahead_pair(rows, "c").transpose(1, 0, 2, 3, 4)
    return rows.reshape((SIDE,) + rows.shape[2:])


def ahead_pair(value, axis):
    other = ahead(value, axis, 1)
    first = lax.axis_index(axis) == 0
    return jnp.stack([jnp.where(first, value, other), jnp.where(first, other, value)])


def whole(block_pos, queries, keys, values, attention_output, output_gradient, log_softmax_norm, features):
    places = block_pos.T
    norm = log_softmax_norm.transpose(1, 0, 2)
    q_own, kv_own = pack(
        places, queries, output_gradient, attention_output, norm, keys, values
    )
    q_all = swap(q_own, "x")
    kv_all = lax.all_gather(kv_own, "zh", axis=0)
    dq, dkv = attention_grads(q_all, kv_all)

    groups = [list(Z_ORDER)]
    dkv = lax.all_to_all(dkv, "zh", 0, 0, tiled=True, axis_index_groups=groups)
    key_copies, key_gradient, value_gradient = fold(dkv)
    here = lax.axis_index("x")
    pieces = [lax.dynamic_index_in_dim(dq, (here + s) % SIDE, 0, keepdims=False) for s in range(SIDE)]
    dq = pieces[:1] + [ahead(pieces[s], "x", s) for s in (1, 2, 3)]
    weights = row_features(features)
    groups = [list(S_ORDER)]
    gathered = lax.all_to_all(key_copies, "s", 0, 0, tiled=True, axis_index_groups=groups)
    partial = weight_products(weights, gathered)
    partial = swap(partial, ("x", "yl", "c"))
    mine = total(partial.reshape((SIDE, SIDE) + partial.shape[1:])).astype(jnp.bfloat16)
    mine = mine.reshape(SIDE, features.shape[-1], HEAD_SIZE)
    mine = lax.all_gather(mine, "zh", axis=0, tiled=True)
    grad_wk, grad_q = finish(mine, dq)
    return (grad_q, key_gradient, value_gradient, grad_wk)


def solution(mesh):
    fine = Mesh(mesh.devices.reshape(4, 4, 8, 2, 2), CTX + FSDP)
    return jax.shard_map(
        whole,
        mesh=fine,
        in_specs=(
            P(None, CTX),
            P(FSDP, CTX, None),
            P(FSDP, CTX, None),
            P(FSDP, CTX, None),
            P(FSDP, CTX, None),
            P(FSDP, CTX, None),
            P(FSDP, None, CTX),
            P(None, CTX, FSDP),
        ),
        out_specs=(P(FSDP, CTX, None), P(FSDP, CTX, None), P(FSDP, CTX, None), P(FSDP, None)),
        check_vma=False,
    )
```

```python
import jax
import jax.numpy as jnp
from jax import lax
from jax.experimental import pallas as pl
from jax.experimental.pallas import tpu as pltpu
from jax.sharding import Mesh
from jax.sharding import PartitionSpec as P


HEADS = 5
HEAD_SIZE = 128
BLOCK = 128
STACK = HEADS * BLOCK
SIDE = 4
SCALE = HEAD_SIZE ** (-0.5)
LOG2E = 1.4426950408889634
CTX = ("x", "zh")
FSDP = ("s", "yl", "c")
GRANT = 16 * 2**20
Z_ORDER = (1, 0, 3, 2)
S_ORDER = (4, 2, 6, 0, 5, 3, 7, 1)
Q_ROWS = 2 * STACK + 32
KV_ROWS = 2 * BLOCK + 16


def dot(a, b, dims):
    return lax.dot_general(a, b, (dims, ((), ())), preferred_element_type=jnp.float32)


def parts_of(value):
    first = value.astype(jnp.bfloat16)
    value = value - first.astype(jnp.float32)
    second = value.astype(jnp.bfloat16)
    value = value - second.astype(jnp.float32)
    return [first.astype(jnp.float32), second.astype(jnp.float32), value]


def own_place(places):
    return places[0, lax.axis_index("s")]


def pack_kernel(places, q_ref, g_ref, o_ref, norm_ref, k_ref, v_ref, q_out, kv_out):
    place = own_place(places)
    deltas = []
    for h in range(HEADS):
        cols = slice(h * HEAD_SIZE, (h + 1) * HEAD_SIZE)
        q = q_ref[0, :, cols]
        g = g_ref[0, :, cols]
        for copy in range(SIDE):
            q_out[copy, h * BLOCK : (h + 1) * BLOCK, :] = q
            q_out[copy, STACK + h * BLOCK : STACK + (h + 1) * BLOCK, :] = g
        product = g.astype(jnp.float32) * o_ref[0, :, cols].astype(jnp.float32)
        deltas.append(jnp.sum(product.T, axis=0, keepdims=True))
    delta = jnp.concatenate(deltas, axis=0)
    norm = norm_ref[:, 0, :] * LOG2E
    tail = jnp.full((2, HEAD_SIZE), place, jnp.int32).astype(jnp.float32)
    extra = jnp.concatenate(parts_of(norm) + parts_of(delta) + [tail], axis=0)
    for copy in range(SIDE):
        q_out[copy, 2 * STACK :, :] = extra.astype(jnp.bfloat16)
    kv_out[:BLOCK, :] = k_ref[0]
    kv_out[BLOCK : 2 * BLOCK, :] = v_ref[0]
    tail = jnp.full((16, HEAD_SIZE), place, jnp.int32)
    kv_out[2 * BLOCK :, :] = tail.astype(jnp.float32).astype(jnp.bfloat16)


def places_of(blocks):
    digits = sum(rows.astype(jnp.float32) * 16.0**j for j, rows in enumerate(blocks))
    word = jnp.max(digits).astype(jnp.int32)
    return [(word >> (4 * j)) & 15 for j in range(len(blocks))]


def attention_kernel(
    q_all, kv_ref, dq_ref, dkv_ref, k_s, v_s, k_t, dk_acc, dv_acc, rank, sorted_place, q_place
):
    dk_acc[...] = jnp.zeros_like(dk_acc)
    dv_acc[...] = jnp.zeros_like(dv_acc)
    key_row = lax.broadcasted_iota(jnp.int32, (BLOCK, STACK), 0)
    query_col = lax.broadcasted_iota(jnp.int32, (BLOCK, STACK), 1) & (BLOCK - 1)
    offset = key_row - query_col
    places = places_of([kv_ref[j, 2 * BLOCK :, :] for j in range(SIDE)])
    tails = [q_all[i, 2 * STACK + 16 :, :].astype(jnp.float32)[14:] for i in range(SIDE)]
    for i, place in enumerate(places_of(tails)):
        q_place[i] = place
    for j in range(SIDE):
        r = sum((places[m] < places[j]).astype(jnp.int32) for m in range(SIDE) if m != j)
        rank[j] = r
        sorted_place[r] = places[j]
        at = pl.multiple_of(r * BLOCK, BLOCK)
        k = kv_ref[j, :BLOCK, :]
        k_s[pl.ds(at, BLOCK), :] = k
        v_s[pl.ds(at, BLOCK), :] = kv_ref[j, BLOCK : 2 * BLOCK, :]
        k_t[r] = k.T

    def row(i, carry):
        q_ref = q_all.at[i]
        extra = q_ref[2 * STACK :, :].astype(jnp.float32)
        norm = extra[0:5] + extra[5:10] + extra[10:15]
        delta = extra[15:20] + extra[20:25] + extra[25:30]
        norm = jnp.concatenate([norm[h : h + 1] for h in range(HEADS)], axis=1)
        delta = jnp.concatenate([delta[h : h + 1] for h in range(HEADS)], axis=1)
        here = q_place[i]
        seen = sum((sorted_place[j] <= here).astype(jnp.int32) for j in range(SIDE))

        @pl.when(seen == 0)
        def _():
            dq_ref[i] = jnp.zeros((HEAD_SIZE, STACK), jnp.bfloat16)

        for count in range(1, SIDE + 1):

            @pl.when(seen == count)
            def _(count=count):
                rows = count * BLOCK
                q = q_ref[:STACK, :]
                g = q_ref[STACK : 2 * STACK, :]
                last = (here - sorted_place[count - 1]) * BLOCK
                scores = dot(k_s[:rows, :], q, ((1,), (1,))) * (SCALE * LOG2E)
                probs = jnp.exp2(scores - norm)
                tail = jnp.where(offset <= last, probs[rows - BLOCK :], 0.0)
                probs = jnp.concatenate([probs[: rows - BLOCK], tail], axis=0) if count > 1 else tail
                dprobs = dot(v_s[:rows, :], g, ((1,), (1,)))
                dscores = (probs * (dprobs - delta) * SCALE).astype(jnp.bfloat16)
                dv_acc[:rows, :] += dot(probs.astype(jnp.bfloat16), g, ((1,), (0,)))
                dk_acc[:rows, :] += dot(dscores, q, ((1,), (0,)))
                k_cols = jnp.concatenate([k_t[j] for j in range(count)], axis=1)
                dq_ref[i] = dot(k_cols, dscores, ((1,), (0,))).astype(jnp.bfloat16)

        return carry

    lax.fori_loop(0, SIDE, row, 0)
    for j in range(SIDE):
        at = pl.multiple_of(rank[j] * BLOCK, BLOCK)
        slot = Z_ORDER.index(j)
        dkv_ref[slot, :BLOCK, :] = dk_acc[pl.ds(at, BLOCK), :].astype(jnp.bfloat16)
        dkv_ref[slot, BLOCK:, :] = dv_acc[pl.ds(at, BLOCK), :].astype(jnp.bfloat16)


def fold_kernel(parts, copies_out, key_out, value_out):
    key = sum(parts[j, :BLOCK, :].astype(jnp.float32) for j in range(SIDE)).astype(jnp.bfloat16)
    for copy in range(8):
        copies_out[copy] = key
    key_out[0] = key
    value = sum(parts[j, BLOCK:, :].astype(jnp.float32) for j in range(SIDE))
    value_out[0] = value.astype(jnp.bfloat16)


def weight_kernel(rows, keys, out_ref):
    keys = keys[...].reshape(8 * BLOCK, HEAD_SIZE)
    for f in range(SIDE):
        left = jnp.concatenate([rows[f, s] for s in S_ORDER], axis=1)
        total = dot(left, keys, ((1,), (0,))).astype(jnp.bfloat16)
        for copy in range(SIDE):
            out_ref[f * SIDE + copy] = total


def finish_kernel(parts, d0, d1, d2, d3, wk_out, q_out):
    for r in range(SIDE):
        total = sum(parts[b * SIDE + r].astype(jnp.float32) for b in range(SIDE))
        wk_out[:, r * HEAD_SIZE : (r + 1) * HEAD_SIZE] = total
    for h in range(HEADS):
        cols = slice(h * HEAD_SIZE, (h + 1) * HEAD_SIZE)
        total = sum(d[:, cols].astype(jnp.float32) for d in (d0, d1, d2, d3))
        q_out[0, :, cols] = total.T.astype(jnp.bfloat16)


SMEM = pl.BlockSpec(memory_space=pltpu.SMEM)
VMEM = pl.BlockSpec(memory_space=pltpu.VMEM)


def struct(shape, dtype=jnp.bfloat16):
    return jax.ShapeDtypeStruct(shape, dtype)


def pack(places, queries, gradient, output, norm, keys, values):
    return pl.pallas_call(
        pack_kernel,
        out_shape=(struct((SIDE, Q_ROWS, HEAD_SIZE)), struct((KV_ROWS, HEAD_SIZE))),
        in_specs=[SMEM] + [VMEM] * 6,
        out_specs=(VMEM, VMEM),
        name="pack",
    )(places, queries, gradient, output, norm, keys, values)


def attention_grads(q_all, kv_all):
    return pl.pallas_call(
        attention_kernel,
        out_shape=(struct((SIDE, HEAD_SIZE, STACK)), struct((SIDE, 2 * BLOCK, HEAD_SIZE))),
        in_specs=[VMEM] * 2,
        out_specs=(VMEM,) * 2,
        scratch_shapes=[
            pltpu.VMEM((SIDE * BLOCK, HEAD_SIZE), jnp.bfloat16),
            pltpu.VMEM((SIDE * BLOCK, HEAD_SIZE), jnp.bfloat16),
            pltpu.VMEM((SIDE, HEAD_SIZE, BLOCK), jnp.bfloat16),
            pltpu.VMEM((SIDE * BLOCK, HEAD_SIZE), jnp.float32),
            pltpu.VMEM((SIDE * BLOCK, HEAD_SIZE), jnp.float32),
            pltpu.SMEM((SIDE,), jnp.int32),
            pltpu.SMEM((SIDE,), jnp.int32),
            pltpu.SMEM((SIDE,), jnp.int32),
        ],
        compiler_params=pltpu.CompilerParams(vmem_limit_bytes=GRANT),
        name="attention_grads",
    )(q_all, kv_all)


def fold(parts):
    block = (1, BLOCK, HEAD_SIZE)
    return pl.pallas_call(
        fold_kernel,
        out_shape=(struct((8, BLOCK, HEAD_SIZE)), struct(block), struct(block)),
        in_specs=[VMEM],
        out_specs=(VMEM,) * 3,
        compiler_params=pltpu.CompilerParams(vmem_limit_bytes=GRANT),
        name="fold",
    )(parts)


def weight_products(rows, keys):
    return pl.pallas_call(
        weight_kernel,
        out_shape=struct((SIDE * SIDE, rows.shape[2], HEAD_SIZE)),
        in_specs=[VMEM] * 2,
        out_specs=VMEM,
        compiler_params=pltpu.CompilerParams(vmem_limit_bytes=GRANT),
        name="weight_products",
    )(rows, keys)


def finish(parts, dq):
    width = parts.shape[1]
    return pl.pallas_call(
        finish_kernel,
        out_shape=(
            struct((width, SIDE * HEAD_SIZE), jnp.float32),
            struct((1, BLOCK, STACK)),
        ),
        in_specs=[VMEM] * 5,
        out_specs=(VMEM,) * 2,
        compiler_params=pltpu.CompilerParams(vmem_limit_bytes=GRANT),
        name="finish",
    )(parts, *dq)


def ahead(value, axis, steps):
    count = lax.axis_size(axis)
    pairs = [(source, (source + steps) % count) for source in range(count)]
    return lax.ppermute(value, axis, pairs)


def swap(value, axis):
    return lax.all_to_all(value, axis, 0, 0, tiled=True)


def row_features(features):
    rows = features.transpose(0, 2, 1)
    rows = ahead_pair(rows, "yl")
    rows = ahead_pair(rows, "c").transpose(1, 0, 2, 3, 4)
    return rows.reshape((SIDE,) + rows.shape[2:])


def ahead_pair(value, axis):
    other = ahead(value, axis, 1)
    first = lax.axis_index(axis) == 0
    return jnp.stack([jnp.where(first, value, other), jnp.where(first, other, value)])


def whole(block_pos, queries, keys, values, attention_output, output_gradient, log_softmax_norm, features):
    places = block_pos.T
    norm = log_softmax_norm.transpose(1, 0, 2)
    q_own, kv_own = pack(
        places, queries, output_gradient, attention_output, norm, keys, values
    )
    q_all = swap(q_own, "x")
    kv_all = lax.all_gather(kv_own, "zh", axis=0)
    dq, dkv = attention_grads(q_all, kv_all)

    groups = [list(Z_ORDER)]
    dkv = lax.all_to_all(dkv, "zh", 0, 0, tiled=True, axis_index_groups=groups)
    key_copies, key_gradient, value_gradient = fold(dkv)
    here = lax.axis_index("x")
    pieces = [lax.dynamic_index_in_dim(dq, (here + s) % SIDE, 0, keepdims=False) for s in range(SIDE)]
    dq = pieces[:1] + [ahead(pieces[s], "x", s) for s in (1, 2, 3)]
    weights = row_features(features)
    groups = [list(S_ORDER)]
    gathered = lax.all_to_all(key_copies, "s", 0, 0, tiled=True, axis_index_groups=groups)
    partial = weight_products(weights, gathered)
    partial = swap(partial, ("yl", "c", "x"))
    partial = partial.reshape((SIDE, SIDE) + partial.shape[1:]).astype(jnp.float32)
    mine = jnp.sum(partial, axis=1).astype(jnp.bfloat16)
    mine = mine.reshape(SIDE, features.shape[-1], HEAD_SIZE)
    mine = lax.all_gather(mine, "zh", axis=0, tiled=True)
    grad_wk, grad_q = finish(mine, dq)
    return (grad_q, key_gradient, value_gradient, grad_wk)


def solution(mesh):
    fine = Mesh(mesh.devices.reshape(4, 4, 8, 2, 2), CTX + FSDP)
    return jax.shard_map(
        whole,
        mesh=fine,
        in_specs=(
            P(None, CTX),
            P(FSDP, CTX, None),
            P(FSDP, CTX, None),
            P(FSDP, CTX, None),
            P(FSDP, CTX, None),
            P(FSDP, CTX, None),
            P(FSDP, None, CTX),
            P(None, CTX, FSDP),
        ),
        out_specs=(P(FSDP, CTX, None), P(FSDP, CTX, None), P(FSDP, CTX, None), P(FSDP, None)),
        check_vma=False,
    )
```
